32 devices in a mesh: req: 8 (over z, y), tp: 4 (over x, core).
Axes of the slice: x: 2, y: 2, z: 4, core: 2. Of those that a mesh axis runs over, the one named last changes fastest.
Arguments:
- hidden: bfloat16 [2048, 5120], P('req', 'tp'), may hold values from -200 to 200
- norm_gain: bfloat16 [5120], replicated, may hold values from 0.099609375 to 1.8984375
- wq: bfloat16 [5120, 4096], P(None, 'tp'), may hold values from -0.078125 to 0.078125
- wkv: bfloat16 [5120, 2, 1024], P(None, None, 'tp'), may hold values from -0.15625 to 0.15625
- wo: bfloat16 [4096, 5120], P('tp'), may hold values from -1 to 1
- perm: int32 [16], replicated, may hold values from 0 to 15, as said below
- prior_len: int32 [16], P('req'), may hold values from 128 to 8192, as said below
- page_table: int32 [16, 64], P('req'), may hold values from 0 to 127, as said below
- pool: bfloat16 [1024, 128, 2, 1024], P('req', None, None, 'tp'), may hold values from -400 to 400
- send_table: int32 [8, 8, 17], P('req'), may hold values from -1 to 129, as said below
Outputs:
- attn_out: bfloat16 [2048, 5120], P('req', 'tp')
- decode_cache: bfloat16 [8, 8, 17, 128, 2, 1024], P('req', None, None, None, None, 'tp')
The draws below stay inside these ranges and needn't reach their ends.
Inputs may be any that keep to these rules, and one draw needn't show every extreme that they name: `perm`: a permutation of the requests. `prior_len`: one request has exactly 8192 cached tokens and another exactly 128. `page_table`: row r names pages of the pool block of the device that holds the dealt slot of request r; the rows of the 2 requests dealt to one device name all different pages. `send_table`: codes l * 65 + p name updated page p of slot l of the sending device, -1 an empty slot; every page p < (lengths + 255) // 128 of each of its slots is named exactly once in the sending device's row, no other page is named, and in every draw some block is full.
All inputs are finite; a program needn't handle non-finite values.
Results may differ from the reference program's by a relative error of at most 0.013.
The reference program's roundings to bfloat16 on the way count: a program that leaves them out, or rounds other values in their place, can miss the bound.
Values may be sent and summed in bfloat16 or wider, within the bound.
A program may use at most 256 MiB of HBM per device.

```python
import math
import jax
import jax.numpy as jnp
from jax import lax

MODEL_WIDTH = 5120
QUERY_HEADS = 32
KEY_VALUE_HEADS = 8
HEAD_SIZE = 128
PAGE_TOKENS = 128
NEW_TOKENS = 128
SLOTS = 2
PRIOR_PAGE_LIMIT = 64
REQUEST_COUNT = 16
BLOCK_PAGE_LIMIT = 17
N_REQ = 8
N_TP = 4


def pool_order(device_key):
    return jax.random.permutation(device_key, SLOTS * PRIOR_PAGE_LIMIT)


def device_order(device_key):
    return jax.random.permutation(device_key, REQUEST_COUNT // SLOTS)


def shared_tables(key):
    base_key = jax.random.fold_in(key, 17)
    devices = REQUEST_COUNT // SLOTS
    dealt_order = jax.random.permutation(jax.random.fold_in(base_key, 1), REQUEST_COUNT).astype(jnp.int32)
    request_lengths = jax.random.randint(jax.random.fold_in(base_key, 2), (REQUEST_COUNT,), PAGE_TOKENS, PRIOR_PAGE_LIMIT * PAGE_TOKENS + 1, dtype=jnp.int32)
    longest = dealt_order[SLOTS - 1]
    shortest = (longest + 1 + jax.random.randint(jax.random.fold_in(base_key, 4), (), 0, REQUEST_COUNT - 1, dtype=jnp.int32)) % REQUEST_COUNT
    request_lengths = request_lengths.at[longest].set(PRIOR_PAGE_LIMIT * PAGE_TOKENS).at[shortest].set(PAGE_TOKENS)
    pool_orders = jax.vmap(pool_order)(jax.random.split(jax.random.fold_in(base_key, 5), devices)).astype(jnp.int32)
    dealt_tables = pool_orders.reshape(REQUEST_COUNT, PRIOR_PAGE_LIMIT)
    inverse = jnp.argsort(dealt_order).astype(jnp.int32)
    table = dealt_tables[inverse]
    dealt_lengths = request_lengths[dealt_order].reshape(devices, SLOTS)
    pages_needed = (dealt_lengths + NEW_TOKENS + PAGE_TOKENS - 1) // PAGE_TOKENS
    code_width = PRIOR_PAGE_LIMIT + 1
    page_ids = jnp.arange(code_width, dtype=jnp.int32)
    is_valid = (page_ids[None, None, :] < pages_needed[:, :, None]).reshape(devices, SLOTS * code_width)
    page_codes = jnp.broadcast_to(jnp.arange(SLOTS * code_width, dtype=jnp.int32)[None, :], (devices, SLOTS * code_width))
    fill_rank = jnp.cumsum(is_valid.astype(jnp.int32), axis=1) - 1
    targets_order = jax.vmap(device_order)(jax.random.split(jax.random.fold_in(base_key, 6), devices)).astype(jnp.int32)
    dest_block = jnp.clip(fill_rank // BLOCK_PAGE_LIMIT, 0, devices - 1)
    target = jnp.take_along_axis(targets_order, dest_block, axis=1) * BLOCK_PAGE_LIMIT + jnp.maximum(fill_rank, 0) % BLOCK_PAGE_LIMIT
    target = jnp.where(is_valid, target, devices * BLOCK_PAGE_LIMIT)
    row_ids = jnp.broadcast_to(jnp.arange(devices, dtype=jnp.int32)[:, None], target.shape)
    sending = jnp.full((devices, devices * BLOCK_PAGE_LIMIT), -1, jnp.int32).at[row_ids, target].set(page_codes, mode='drop')
    return (dealt_order, request_lengths, table, sending.reshape(devices, devices, BLOCK_PAGE_LIMIT))


def draw_perm(key, part):
    return shared_tables(key)[0]


def draw_prior_len(key, part):
    return shared_tables(key)[1]


def draw_page_table(key, part):
    return shared_tables(key)[2]


def draw_send_table(key, part):
    return shared_tables(key)[3]


def draw_hidden(key, part):
    key_one = jax.random.fold_in(key, 0)
    page_dimensions = (REQUEST_COUNT * NEW_TOKENS, MODEL_WIDTH)
    column = jnp.arange(MODEL_WIDTH, dtype=jnp.float32) / MODEL_WIDTH
    base_values = jnp.clip(jax.random.normal(key_one, page_dimensions, jnp.float32), -6.0, 6.0)
    values = base_values * jnp.power(3.0, 0.5 * column)[None, :]
    return values.astype(jnp.bfloat16)


def draw_pool(key, part):
    key_one = jax.random.fold_in(key, 0)
    page_dimensions = (REQUEST_COUNT * PRIOR_PAGE_LIMIT, PAGE_TOKENS, 2, KEY_VALUE_HEADS * HEAD_SIZE)
    plane_index = jnp.arange(2, dtype=jnp.int32)[None, None, :, None]
    plane_scale = jnp.where(plane_index == 0, 1.5, 1.0)
    values = jnp.clip(jax.random.normal(key_one, page_dimensions, jnp.float32), -6.0, 6.0) * plane_scale
    return values.astype(jnp.bfloat16)


def level_of(stream_key, shape, cuts, low, largest):
    factor_of = 1.0
    for dim, blocks in cuts:
        heights = jax.random.uniform(jax.random.fold_in(jax.random.fold_in(stream_key, 6), dim), (blocks,), jnp.float32, low / len(cuts), largest / len(cuts))
        factor_of = factor_of * jnp.repeat(jnp.exp(heights), shape[dim] // blocks).reshape((-1,) + (1,) * (len(shape) - 1 - dim))
    return factor_of


def noise(rng, dims, deviation, limit, cuts=(), kind=jnp.bfloat16):
    level = level_of(rng, dims, cuts, -0.22, 0.18) if cuts else 1.0
    drawn = jax.random.normal(rng, dims, jnp.float32) * deviation * level
    return jnp.minimum(jnp.maximum(drawn, -limit), limit).astype(kind)


def setup_inputs(seed: int = 0) -> dict:
    key_list = jax.random.split(jax.random.key(seed), 11)
    return {
        "hidden": draw_hidden(jax.random.fold_in(key_list[10], 71), 0),
        "norm_gain": jnp.clip(1.0 + 0.18 * jax.random.normal(key_list[1], (MODEL_WIDTH,), jnp.float32), 0.099609375, 1.8984375).astype(jnp.bfloat16),
        "wq": noise(key_list[2], (MODEL_WIDTH, QUERY_HEADS * HEAD_SIZE), MODEL_WIDTH ** -0.5, 0.078125, ((1, 4),)),
        "wkv": noise(key_list[3], (MODEL_WIDTH, 2, KEY_VALUE_HEADS * HEAD_SIZE), (MODEL_WIDTH // 4) ** -0.5, 0.15625, ((2, 4),)),
        "wo": noise(key_list[4], (QUERY_HEADS * HEAD_SIZE, MODEL_WIDTH), (HEAD_SIZE // 4) ** -0.5, 1.0, ((0, 4),)),
        "perm": draw_perm(jax.random.fold_in(key_list[10], 71), 0),
        "prior_len": draw_prior_len(jax.random.fold_in(key_list[10], 71), 0),
        "page_table": draw_page_table(jax.random.fold_in(key_list[10], 71), 0),
        "pool": draw_pool(jax.random.fold_in(key_list[10], 71), 0),
        "send_table": draw_send_table(jax.random.fold_in(key_list[10], 71), 0),
    }


NORM_EPSILON = 1e-05
ROPE_THETA = 100000000.0

def normalize(rows, gain):
    wide_rows = rows.astype(jnp.float32)
    mean_square = lax.optimization_barrier(jnp.mean(wide_rows * wide_rows, axis=-1, keepdims=True))
    return (wide_rows * lax.rsqrt(mean_square + NORM_EPSILON) * gain.astype(jnp.float32)).astype(jnp.bfloat16)

def rotate(vectors, positions):
    half_size = vectors.shape[-1] // 2
    frequency = jnp.power(jnp.float32(ROPE_THETA), -2.0 * jnp.arange(half_size, dtype=jnp.float32) / vectors.shape[-1])
    angles = positions.astype(jnp.float32)[:, None] * frequency[None, :]
    cosine = jnp.cos(angles)[:, None, :]
    sine_part = jnp.sin(angles)[:, None, :]
    first_half = vectors[..., :half_size]
    second_half = vectors[..., half_size:]
    return jnp.concatenate([first_half * cosine - second_half * sine_part, second_half * cosine + first_half * sine_part], axis=-1)

def reference(hidden, norm_gain, wq, wkv, wo, perm, prior_len, page_table, pool, send_table):
    request_lengths = prior_len[perm]
    page_tables = page_table[perm]
    normalized_input = normalize(hidden, norm_gain)
    query_proj = jnp.dot(normalized_input, wq, preferred_element_type=jnp.float32)
    key_value_projection = jnp.dot(normalized_input, wkv.reshape(MODEL_WIDTH, 2 * KEY_VALUE_HEADS * HEAD_SIZE), preferred_element_type=jnp.float32)
    positions = (request_lengths[:, None] + jnp.arange(NEW_TOKENS, dtype=jnp.int32)[None, :]).reshape(-1)
    query_vectors = rotate(query_proj.reshape(-1, QUERY_HEADS, HEAD_SIZE), positions).astype(jnp.bfloat16)
    key_value_heads = key_value_projection.reshape(-1, 2, KEY_VALUE_HEADS, HEAD_SIZE)
    incoming_keys = rotate(key_value_heads[:, 0], positions).astype(jnp.bfloat16)
    incoming_values = key_value_heads[:, 1].astype(jnp.bfloat16)

    def single_slot(packed):
        query_slots, slot_keys, slot_values, length, table_row, slot_id = packed
        base_page = slot_id // SLOTS * (SLOTS * PRIOR_PAGE_LIMIT)
        cached_entries = pool[base_page + table_row]
        stored_keys = cached_entries[:, :, 0].reshape(PRIOR_PAGE_LIMIT * PAGE_TOKENS, KEY_VALUE_HEADS, HEAD_SIZE)
        stored_values = cached_entries[:, :, 1].reshape(PRIOR_PAGE_LIMIT * PAGE_TOKENS, KEY_VALUE_HEADS, HEAD_SIZE)
        all_keys = jnp.concatenate([stored_keys, slot_keys], axis=0).astype(jnp.float32)
        all_values = jnp.concatenate([stored_values, slot_values], axis=0).astype(jnp.float32)
        cached_ok = jnp.arange(PRIOR_PAGE_LIMIT * PAGE_TOKENS, dtype=jnp.int32) < length
        token_ids = jnp.arange(NEW_TOKENS, dtype=jnp.int32)
        causal = token_ids[None, :] <= token_ids[:, None]
        valid = jnp.concatenate([jnp.broadcast_to(cached_ok[None, :], (NEW_TOKENS, PRIOR_PAGE_LIMIT * PAGE_TOKENS)), causal], axis=1)
        grouped_queries = query_slots.reshape(NEW_TOKENS, KEY_VALUE_HEADS, QUERY_HEADS // KEY_VALUE_HEADS, HEAD_SIZE).astype(jnp.float32)
        scores = jnp.einsum('tgjd,kgd->gjtk', grouped_queries, all_keys) / math.sqrt(HEAD_SIZE)
        masked = jnp.where(valid, scores, -1e+30)
        highest = lax.optimization_barrier(jnp.max(masked, axis=-1, keepdims=True))
        weights = jnp.where(valid, jnp.exp(masked - highest), 0.0)
        rounded = lax.optimization_barrier(weights.astype(jnp.bfloat16))
        numer = jnp.einsum('gjtk,kgd->gjtd', rounded.astype(jnp.float32), all_values)
        context = numer / lax.optimization_barrier(jnp.sum(weights, axis=-1))[..., None]
        return context.transpose(2, 0, 1, 3).reshape(NEW_TOKENS, QUERY_HEADS * HEAD_SIZE).astype(jnp.bfloat16)
    context_rows = lax.map(single_slot, (query_vectors.reshape(REQUEST_COUNT, NEW_TOKENS, QUERY_HEADS, HEAD_SIZE), incoming_keys.reshape(REQUEST_COUNT, NEW_TOKENS, KEY_VALUE_HEADS, HEAD_SIZE), incoming_values.reshape(REQUEST_COUNT, NEW_TOKENS, KEY_VALUE_HEADS, HEAD_SIZE), request_lengths, page_tables, jnp.arange(REQUEST_COUNT, dtype=jnp.int32)))
    context = context_rows.reshape(REQUEST_COUNT * NEW_TOKENS, QUERY_HEADS * HEAD_SIZE)
    group_width = QUERY_HEADS * HEAD_SIZE // N_TP
    total = jnp.zeros((REQUEST_COUNT * NEW_TOKENS, MODEL_WIDTH), jnp.float32)
    for group in range(N_TP):
        term = jnp.dot(context[:, group * group_width:(group + 1) * group_width], wo[group * group_width:(group + 1) * group_width], preferred_element_type=jnp.float32).astype(jnp.bfloat16)
        term = lax.optimization_barrier(term)
        total = total + term.astype(jnp.float32)
    attn_out = total.astype(jnp.bfloat16)
    recent_rows = jnp.stack([incoming_keys.reshape(REQUEST_COUNT, NEW_TOKENS, KEY_VALUE_HEADS * HEAD_SIZE), incoming_values.reshape(REQUEST_COUNT, NEW_TOKENS, KEY_VALUE_HEADS * HEAD_SIZE)], axis=2)

    def one_target(entries):
        flat_codes = entries.reshape(-1)
        is_valid = flat_codes >= 0
        clean_codes = jnp.maximum(flat_codes, 0)
        sources = jnp.repeat(jnp.arange(N_REQ, dtype=jnp.int32), BLOCK_PAGE_LIMIT)
        slot_ids = sources * SLOTS + clean_codes // (PRIOR_PAGE_LIMIT + 1)
        page_index = clean_codes % (PRIOR_PAGE_LIMIT + 1)
        slot_lengths = request_lengths[slot_ids]
        physical = slot_ids // SLOTS * (SLOTS * PRIOR_PAGE_LIMIT) + page_tables[slot_ids, jnp.minimum(page_index, PRIOR_PAGE_LIMIT - 1)]
        token_pos = page_index[:, None] * PAGE_TOKENS + jnp.arange(PAGE_TOKENS, dtype=jnp.int32)[None, :]
        keep_mask = is_valid[:, None] & (token_pos < slot_lengths[:, None])
        page_contents = jnp.where(keep_mask[:, :, None, None], pool[physical], jnp.zeros((), pool.dtype))
        offsets = token_pos - slot_lengths[:, None]
        inside = is_valid[:, None] & (offsets >= 0) & (offsets < NEW_TOKENS)
        picked = recent_rows[slot_ids[:, None], jnp.clip(offsets, 0, NEW_TOKENS - 1)]
        page_contents = jnp.where(inside[:, :, None, None], picked, page_contents)
        return page_contents.reshape(N_REQ, BLOCK_PAGE_LIMIT, PAGE_TOKENS, 2, KEY_VALUE_HEADS * HEAD_SIZE)
    decode_cache = lax.map(one_target, jnp.transpose(send_table, (1, 0, 2)))
    return (attn_out, decode_cache)
```

```python
import math

import jax
import jax.numpy as jnp
from jax import lax
from jax.experimental import pallas as pl
from jax.experimental.pallas import tpu as pltpu
from jax.sharding import PartitionSpec as P

HEAD_SIZE = 128
NORM_EPSILON = 1e-05
ROPE_THETA = 100000000.0
BLOCK_PAGES = 4


def normalize(rows, gain):
    wide_rows = rows.astype(jnp.float32)
    mean_square = jnp.mean(wide_rows * wide_rows, axis=-1, keepdims=True)
    return (wide_rows * lax.rsqrt(mean_square + NORM_EPSILON) * gain.astype(jnp.float32)).astype(
        jnp.bfloat16
    )


def rotate(vectors, positions):
    half_size = vectors.shape[-1] // 2
    frequency = jnp.power(
        jnp.float32(ROPE_THETA), -2.0 * jnp.arange(half_size, dtype=jnp.float32) / vectors.shape[-1]
    )
    angles = positions.astype(jnp.float32)[:, None] * frequency[None, :]
    cosine = jnp.cos(angles)[:, None, :]
    sine_part = jnp.sin(angles)[:, None, :]
    first_half = vectors[..., :half_size]
    second_half = vectors[..., half_size:]
    return jnp.concatenate(
        [
            first_half * cosine - second_half * sine_part,
            second_half * cosine + first_half * sine_part,
        ],
        axis=-1,
    )


class Layout:
    def __init__(self, slots, row_pages, peers, block):
        self.slots, self.row_pages, self.peers, self.block = slots, row_pages, peers, block
        self.code_width = row_pages + 1
        self.sends = slots + slots * row_pages
        self.width = self.sends + peers * block

    def request(self, perm, device, slot):
        request = perm[device * self.slots + slot]
        return (request // self.slots) * self.width, request % self.slots

    def length(self, table, perm, device, slot):
        base, row = self.request(perm, device, slot)
        return table[base + row]

    def physical(self, table, perm, device, slot, page):
        base, row = self.request(perm, device, slot)
        return table[base + self.slots + row * self.row_pages + jnp.minimum(page, self.row_pages - 1)]

    def code(self, table, source, target, number):
        return table[source * self.width + self.sends + target * self.block + number]


def pack_kernel(layout, table, perm, me, pool, out, sem):
    def send(index, carry):
        target, number = index // layout.block, index % layout.block
        code = jnp.maximum(layout.code(table, me[0], target, number), 0)
        page = layout.physical(
            table, perm, me[0], code // layout.code_width, code % layout.code_width
        )
        pltpu.make_async_copy(pool.at[page], out.at[target, number], sem).start()
        return carry

    lax.fori_loop(0, layout.peers * layout.block, send, 0)
    pltpu.make_async_copy(out, out, sem).wait()


def pack_pages(layout, table, perm, me, pool):
    return pl.pallas_call(
        lambda *refs: pack_kernel(layout, *refs),
        out_shape=jax.ShapeDtypeStruct((layout.peers, layout.block) + pool.shape[1:], pool.dtype),
        grid_spec=pltpu.PrefetchScalarGridSpec(
            num_scalar_prefetch=3,
            grid=(1,),
            in_specs=[pl.BlockSpec(memory_space=pl.ANY)],
            out_specs=pl.BlockSpec(memory_space=pl.ANY),
            scratch_shapes=[pltpu.SemaphoreType.DMA],
        ),
        name="pack_pages",
    )(table, perm, me, pool)


def finish_kernel(layout, table, perm, me, arrived, recent, zeros, out, sem):
    page_len = out.shape[2]

    def rows(source, source_row, target, target_row, count):
        size = page_len
        while size:
            offset = count // (2 * size) * (2 * size)

            @pl.when(count // size % 2 == 1)
            def _(size=size, offset=offset):
                pltpu.make_async_copy(
                    source.at[pl.ds(source_row + offset, size)],
                    target.at[pl.ds(target_row + offset, size)],
                    sem,
                ).start()

            size //= 2

    def place(index, carry):
        source, number = index // layout.block, index % layout.block
        raw_code = layout.code(table, source, me[0], number)
        code = jnp.maximum(raw_code, 0)
        slot, page = code // layout.code_width, code % layout.code_width
        length = layout.length(table, perm, source, slot)
        full, kept = length // page_len, length % page_len
        target = out.at[source, number]
        valid = raw_code >= 0

        @pl.when(valid & (page < full))
        def _():
            pltpu.make_async_copy(arrived.at[source, number], target, sem).start()

        @pl.when(jnp.logical_not(valid) | (page > full + 1))
        def _():
            pltpu.make_async_copy(zeros, target, sem).start()

        @pl.when(valid & (page == full))
        def _():
            rows(arrived.at[source, number], 0, target, 0, kept)
            rows(recent.at[source, slot], 0, target, kept, page_len - kept)

        @pl.when(valid & (page == full + 1))
        def _():
            rows(recent.at[source, slot], page_len - kept, target, 0, kept)
            rows(zeros, 0, target, kept, page_len - kept)

        return carry

    lax.fori_loop(0, layout.peers * layout.block, place, 0)
    pltpu.make_async_copy(out, out, sem).wait()


def finish_pages(layout, table, perm, me, arrived, recent):
    zeros = jnp.zeros(arrived.shape[2:], arrived.dtype)
    return pl.pallas_call(
        lambda *refs: finish_kernel(layout, *refs),
        out_shape=jax.ShapeDtypeStruct(arrived.shape, arrived.dtype),
        grid_spec=pltpu.PrefetchScalarGridSpec(
            num_scalar_prefetch=3,
            grid=(1,),
            in_specs=[pl.BlockSpec(memory_space=pl.ANY)] * 3,
            out_specs=pl.BlockSpec(memory_space=pl.ANY),
            scratch_shapes=[pltpu.SemaphoreType.DMA],
        ),
        name="finish_pages",
    )(table, perm, me, arrived, recent, zeros)


def attend_kernel(lengths, tables, q_ref, nk_ref, nv_ref, *rest):
    k_refs, v_refs = rest[:BLOCK_PAGES], rest[BLOCK_PAGES : 2 * BLOCK_PAGES]
    out_ref, q_rows, top, total, acc = rest[2 * BLOCK_PAGES :]
    kv_heads, rows, head = q_rows.shape
    tokens = q_ref.shape[0]
    groups = rows // tokens
    slot, step = pl.program_id(0), pl.program_id(1)
    page_len = k_refs[0].shape[1]
    block_keys = BLOCK_PAGES * page_len
    length = lengths[slot]
    inv_scale = 1.0 / math.sqrt(head)

    def score(kv, keys):
        return (
            lax.dot_general(
                q_rows[kv], keys, (((1,), (1,)), ((), ())), preferred_element_type=jnp.float32
            )
            * inv_scale
        )

    @pl.when(step == 0)
    def _():
        for kv in range(kv_heads):
            columns = slice(kv * head, (kv + 1) * head)
            for group in range(groups):
                lane = (kv * groups + group) * head
                q_rows[kv, group * tokens : (group + 1) * tokens, :] = q_ref[:, lane : lane + head]
            scores = score(kv, nk_ref[:, columns])
            query_id = lax.broadcasted_iota(jnp.int32, scores.shape, 0) % tokens
            key_id = lax.broadcasted_iota(jnp.int32, scores.shape, 1)
            scores = jnp.where(key_id <= query_id, scores, -1e30)
            highest = jnp.max(scores, axis=-1, keepdims=True)
            weights = jnp.exp(scores - highest)
            top[kv] = jnp.broadcast_to(highest, (rows, head))
            total[kv] = jnp.broadcast_to(jnp.sum(weights, axis=-1, keepdims=True), (rows, head))
            acc[kv] = jnp.dot(
                weights.astype(jnp.bfloat16), nv_ref[:, columns], preferred_element_type=jnp.float32
            )

    @pl.when(step * block_keys < length)
    def _():
        for kv in range(kv_heads):
            columns = slice(kv * head, (kv + 1) * head)
            keys = jnp.concatenate([ref[0, :, columns] for ref in k_refs], axis=0)
            values = jnp.concatenate([ref[0, :, columns] for ref in v_refs], axis=0)
            scores = score(kv, keys)
            key_id = lax.broadcasted_iota(jnp.int32, scores.shape, 1)
            scores = jnp.where(key_id < length - step * block_keys, scores, -1e30)
            before = top[kv]
            highest = jnp.maximum(before, jnp.max(scores, axis=-1, keepdims=True))
            factor = jnp.exp(before - highest)
            weights = jnp.exp(scores - highest[:, :1])
            top[kv] = highest
            total[kv] = total[kv] * factor + jnp.sum(weights, axis=-1, keepdims=True)
            acc[kv] = acc[kv] * factor + jnp.dot(
                weights.astype(jnp.bfloat16), values, preferred_element_type=jnp.float32
            )

    @pl.when(step == pl.num_programs(1) - 1)
    def _():
        for kv in range(kv_heads):
            context = (acc[kv] / total[kv]).astype(jnp.bfloat16)
            for group in range(groups):
                lane = (kv * groups + group) * head
                out_ref[:, lane : lane + head] = context[group * tokens : (group + 1) * tokens]


def attend(lengths, tables, queries, new_keys, new_values, k_pool, v_pool):
    slots, row_pages = tables.shape
    tokens = queries.shape[0] // slots
    page_len, features = k_pool.shape[1:]
    kv_heads = features // HEAD_SIZE
    rows = tokens * (queries.shape[1] // features)
    steps = row_pages // BLOCK_PAGES

    def page_spec(number):
        def pick(slot, step, lengths, tables):
            last = (lengths[slot] + page_len - 1) // page_len - 1
            return (tables[slot * row_pages + jnp.minimum(step * BLOCK_PAGES + number, last)], 0, 0)

        return pl.BlockSpec((1, page_len, features), pick)

    def slot_rows(slot, step, lengths, tables):
        return (slot, 0)

    pages = [page_spec(number) for number in range(BLOCK_PAGES)]
    state = pltpu.VMEM((kv_heads, rows, HEAD_SIZE), jnp.float32)
    return pl.pallas_call(
        attend_kernel,
        out_shape=jax.ShapeDtypeStruct(queries.shape, jnp.bfloat16),
        grid_spec=pltpu.PrefetchScalarGridSpec(
            num_scalar_prefetch=2,
            grid=(slots, steps),
            in_specs=[
                pl.BlockSpec((tokens, queries.shape[1]), slot_rows),
                pl.BlockSpec((tokens, features), slot_rows),
                pl.BlockSpec((tokens, features), slot_rows),
            ]
            + pages
            + pages,
            out_specs=pl.BlockSpec((tokens, queries.shape[1]), slot_rows),
            scratch_shapes=[
                pltpu.VMEM((kv_heads, rows, HEAD_SIZE), jnp.bfloat16),
                state,
                state,
                state,
            ],
        ),
        compiler_params=pltpu.CompilerParams(
            dimension_semantics=("arbitrary", "arbitrary"), vmem_limit_bytes=40 << 20
        ),
        name="attend",
    )(
        lengths,
        tables.reshape(-1),
        queries,
        new_keys,
        new_values,
        *([k_pool] * BLOCK_PAGES),
        *([v_pool] * BLOCK_PAGES),
    )


def shards(hidden, norm_gain, wq, wkv, wo, perm, prior_len, page_table, pool, send_table):
    slots = prior_len.shape[0]
    tokens = hidden.shape[0] // slots
    _, peers, block = send_table.shape
    layout = Layout(slots, page_table.shape[1], peers, block)
    features = pool.shape[-1]
    device = lax.axis_index("req")
    me = device.astype(jnp.int32).reshape(1)
    mine = jnp.concatenate([prior_len, page_table.reshape(-1), send_table.reshape(-1)])
    table = lax.all_gather(mine, "req", axis=0, tiled=True)
    outgoing = pack_pages(layout, table, perm, me, pool)
    arrived = lax.all_to_all(outgoing, "req", split_axis=0, concat_axis=0, tiled=True)

    full_rows = lax.all_gather(hidden, "tp", axis=1, tiled=True)
    late_pool, wkv, outgoing = lax.optimization_barrier((pool, wkv, outgoing))
    requests = lax.dynamic_slice_in_dim(perm, device * slots, slots)
    by_device = table.reshape(peers, layout.width)
    lengths = by_device[:, :slots].reshape(-1)[requests]
    tables = by_device[:, slots : layout.sends].reshape(-1, layout.row_pages)[requests]

    normalized_input = normalize(full_rows, norm_gain)
    query_proj = jnp.dot(normalized_input, wq, preferred_element_type=jnp.float32)
    pair_proj = jnp.dot(
        normalized_input, wkv.reshape(wkv.shape[0], -1), preferred_element_type=jnp.float32
    )
    positions = (lengths[:, None] + jnp.arange(tokens, dtype=jnp.int32)[None, :]).reshape(-1)
    queries = rotate(query_proj.reshape(query_proj.shape[0], -1, HEAD_SIZE), positions).astype(
        jnp.bfloat16
    )
    pair_heads = pair_proj.reshape(pair_proj.shape[0], 2, -1, HEAD_SIZE)
    new_keys = rotate(pair_heads[:, 0], positions).astype(jnp.bfloat16).reshape(-1, features)
    new_values = pair_heads[:, 1].astype(jnp.bfloat16).reshape(-1, features)
    recent = jnp.stack([new_keys, new_values], axis=1).reshape(slots, tokens, 2, features)
    all_recent = lax.all_gather(recent, "req", axis=0)

    context = attend(
        lengths,
        tables,
        queries.reshape(queries.shape[0], -1),
        new_keys,
        new_values,
        late_pool[:, :, 0],
        late_pool[:, :, 1],
    )
    partial_value = jnp.dot(context, wo, preferred_element_type=jnp.float32)
    attn_out = lax.psum_scatter(
        partial_value.astype(jnp.bfloat16), "tp", scatter_dimension=1, tiled=True
    )
    decode_pages = finish_pages(layout, table, perm, me, arrived, all_recent)
    return (attn_out, decode_pages[None])


def solution(mesh):
    placed = (
        P("req", "tp"),
        P(),
        P(None, "tp"),
        P(None, None, "tp"),
        P("tp", None),
        P(),
        P("req"),
        P("req", None),
        P("req", None, None, "tp"),
        P("req", None, None),
    )
    return jax.shard_map(
        shards,
        mesh=mesh,
        in_specs=placed,
        out_specs=(P("req", "tp"), P("req", None, None, None, None, "tp")),
        check_vma=False,
    )
```

```python
import math

import jax
import jax.numpy as jnp
from jax import lax
from jax.experimental import pallas as pl
from jax.experimental.pallas import tpu as pltpu
from jax.sharding import PartitionSpec as P

HEAD_SIZE = 128
NORM_EPSILON = 1e-05
ROPE_THETA = 100000000.0
BLOCK_PAGES = 4


def normalize(rows, gain):
    wide_rows = rows.astype(jnp.float32)
    mean_square = jnp.mean(wide_rows * wide_rows, axis=-1, keepdims=True)
    return (wide_rows * lax.rsqrt(mean_square + NORM_EPSILON) * gain.astype(jnp.float32)).astype(
        jnp.bfloat16
    )


def rotate(vectors, positions):
    half_size = vectors.shape[-1] // 2
    frequency = jnp.power(
        jnp.float32(ROPE_THETA), -2.0 * jnp.arange(half_size, dtype=jnp.float32) / vectors.shape[-1]
    )
    angles = positions.astype(jnp.float32)[:, None] * frequency[None, :]
    cosine = jnp.cos(angles)[:, None, :]
    sine_part = jnp.sin(angles)[:, None, :]
    first_half = vectors[..., :half_size]
    second_half = vectors[..., half_size:]
    return jnp.concatenate(
        [
            first_half * cosine - second_half * sine_part,
            second_half * cosine + first_half * sine_part,
        ],
        axis=-1,
    )


class Layout:
    def __init__(self, slots, row_pages, peers, block):
        self.slots, self.row_pages, self.peers, self.block = slots, row_pages, peers, block
        self.code_width = row_pages + 1
        self.sends = slots + slots * row_pages
        self.used = self.sends + peers * block
        self.width = -(-self.used // 1024) * 1024
        self.late = 2 * slots
        self.early = block - self.late

    def request(self, perm, device, slot):
        request = perm[device * self.slots + slot]
        return lax.div(request, self.slots) * self.width, lax.rem(request, self.slots)

    def length(self, table, perm, device, slot):
        base, row = self.request(perm, device, slot)
        return table[base + row]

    def physical(self, table, perm, device, slot, page):
        base, row = self.request(perm, device, slot)
        return table[base + self.slots + row * self.row_pages + jnp.minimum(page, self.row_pages - 1)]

    def split(self, code):
        return lax.div(code, self.code_width), lax.rem(code, self.code_width)

    def visit(self, table, perm, source, target, page_len, use):
        whole = [
            lax.div(self.length(table, perm, source, slot), page_len) for slot in range(self.slots)
        ]
        base = source * self.width + self.sends + target * self.block

        def step(number, counts):
            plain, tails = counts
            code = table[base + number]
            valid = code >= 0
            slot, page = self.split(jnp.maximum(code, 0))
            first = whole[0]
            for other in range(1, self.slots):
                first = jnp.where(slot == other, whole[other], first)
            tail = valid & (page >= first)
            place = jnp.where(valid, jnp.where(tail, self.block - 1 - tails, plain), -1)
            use(number, code, place)
            return (
                plain + jnp.where(valid & jnp.logical_not(tail), 1, 0),
                tails + jnp.where(tail, 1, 0),
            )

        lax.fori_loop(0, self.block, step, (jnp.int32(0), jnp.int32(0)))


def exchange_kernel(peers, mine, out, send_sems, recv_sems):
    me = lax.axis_index("req")
    barrier = pltpu.get_barrier_semaphore()
    for hop in range(1, peers):
        pl.semaphore_signal(
            barrier,
            inc=1,
            device_id={"req": lax.rem(me + hop, peers)},
            device_id_type=pl.DeviceIdType.MESH,
        )
    pl.semaphore_wait(barrier, peers - 1)
    copies = []
    for hop in range(1, peers):
        copy = pltpu.make_async_remote_copy(
            src_ref=mine,
            dst_ref=out.at[me],
            send_sem=send_sems.at[hop - 1],
            recv_sem=recv_sems.at[hop - 1],
            device_id={"req": lax.rem(me + hop, peers)},
            device_id_type=pl.DeviceIdType.MESH,
        )
        copy.start()
        copies.append(copy)
    out[me] = mine[...]
    for copy in copies:
        copy.wait()


def exchange(peers, mine):
    return pl.pallas_call(
        lambda *refs: exchange_kernel(peers, *refs),
        out_shape=jax.ShapeDtypeStruct((peers,) + mine.shape, mine.dtype),
        in_specs=[pl.BlockSpec(memory_space=pltpu.VMEM)],
        out_specs=pl.BlockSpec(memory_space=pltpu.VMEM),
        scratch_shapes=[
            pltpu.SemaphoreType.DMA((peers - 1,)),
            pltpu.SemaphoreType.DMA((peers - 1,)),
        ],
        compiler_params=pltpu.CompilerParams(collective_id=0, has_side_effects=True),
        name="exchange",
    )(mine)


BUFFERS = 16
AHEAD = 8


def ring(count, load, store, drain):
    def step(index, carry):
        @pl.when(index < count)
        def _():
            @pl.when(index >= BUFFERS)
            def _():
                drain(index - BUFFERS)

            load(index)

        @pl.when(index >= AHEAD)
        def _():
            store(index - AHEAD)

        return carry

    lax.fori_loop(0, count + AHEAD, step, 0)

    def last(index, carry):
        drain(index)
        return carry

    lax.fori_loop(max(count - BUFFERS, 0), count, last, 0)


def copy_rows(source, source_row, target, target_row, count, sem):
    size = target.shape[0]
    while size:
        offset = lax.div(count, 2 * size) * (2 * size)

        @pl.when(lax.rem(lax.div(count, size), 2) == 1)
        def _(size=size, offset=offset):
            pltpu.make_async_copy(
                source.at[pl.ds(source_row + offset, size)],
                target.at[pl.ds(target_row + offset, size)],
                sem,
            ).start()

        size //= 2


def pack_kernel(layout, late, table, perm, me, pool, *rest):
    if late:
        recent, zeros, out, codes, buffers, in_sems, out_sems = rest
    else:
        out, codes, buffers, in_sems, out_sems = rest
    page_len = buffers.shape[1]
    span = layout.late if late else layout.early
    start = layout.early if late else 0
    count = layout.peers * span

    def clear(index, carry):
        codes[index] = 0
        return carry

    lax.fori_loop(0, layout.peers * layout.block, clear, 0)

    def block(target, carry):
        def use(number, code, place):
            @pl.when(place >= 0)
            def _():
                codes[target * layout.block + place] = code

        layout.visit(table, perm, me[0], target, page_len, use)
        return carry

    lax.fori_loop(0, layout.peers, block, 0)

    def load(index):
        spot = lax.rem(index, BUFFERS)
        code = codes[lax.div(index, span) * layout.block + start + lax.rem(index, span)]
        slot, page = layout.split(code)
        cached = pool.at[layout.physical(table, perm, me[0], slot, page)]
        target, sem = buffers.at[spot], in_sems.at[spot]
        if not late:
            pltpu.make_async_copy(cached, target, sem).start()
            return
        length = layout.length(table, perm, me[0], slot)
        full, kept = lax.div(length, page_len), lax.rem(length, page_len)

        @pl.when(page < full)
        def _():
            pltpu.make_async_copy(cached, target, sem).start()

        @pl.when(page == full)
        def _():
            copy_rows(cached, 0, target, 0, kept, sem)
            copy_rows(recent.at[slot], 0, target, kept, page_len - kept, sem)

        @pl.when(page > full)
        def _():
            copy_rows(recent.at[slot], page_len - kept, target, 0, kept, sem)
            copy_rows(zeros, 0, target, kept, page_len - kept, sem)

    def outward(index):
        spot = lax.rem(index, BUFFERS)
        target = out.at[lax.div(index, span), lax.rem(index, span)]
        return pltpu.make_async_copy(buffers.at[spot], target, out_sems.at[spot])

    def store(index):
        spot = lax.rem(index, BUFFERS)
        pltpu.make_async_copy(pool.at[0], buffers.at[spot], in_sems.at[spot]).wait()
        outward(index).start()

    ring(count, load, store, lambda index: outward(index).wait())


def scratch(layout, pool):
    return [
        pltpu.SMEM((layout.peers * layout.block,), jnp.int32),
        pltpu.VMEM((BUFFERS,) + pool.shape[-3:], pool.dtype),
        pltpu.SemaphoreType.DMA((BUFFERS,)),
        pltpu.SemaphoreType.DMA((BUFFERS,)),
    ]


def pack_pages(layout, table, perm, me, pool, *fresh):
    late = bool(fresh)
    span = layout.late if late else layout.early
    return pl.pallas_call(
        lambda *refs: pack_kernel(layout, late, *refs),
        out_shape=jax.ShapeDtypeStruct((layout.peers, span) + pool.shape[1:], pool.dtype),
        grid_spec=pltpu.PrefetchScalarGridSpec(
            num_scalar_prefetch=3,
            grid=(1,),
            in_specs=[pl.BlockSpec(memory_space=pl.ANY)] * (1 + len(fresh)),
            out_specs=pl.BlockSpec(memory_space=pl.ANY),
            scratch_shapes=scratch(layout, pool),
        ),
        name="pack_late" if late else "pack_early",
    )(table, perm, me, pool, *fresh)


def place_kernel(layout, table, perm, me, arrived, zeros, out, places, buffers, in_sems, out_sems, blank, blank_sem):
    page_len = buffers.shape[1]
    fill = pltpu.make_async_copy(zeros, blank, blank_sem)
    fill.start()

    def block(source, carry):
        def use(number, code, place):
            places[source * layout.block + number] = place

        layout.visit(table, perm, source, me[0], page_len, use)
        return carry

    lax.fori_loop(0, layout.peers, block, 0)
    fill.wait()

    def inward(index):
        spot = lax.rem(index, BUFFERS)
        place = jnp.clip(places[index], 0, layout.early - 1)
        return pltpu.make_async_copy(
            arrived.at[lax.div(index, layout.block), place], buffers.at[spot], in_sems.at[spot]
        )

    def outward(index, held):
        target = out.at[lax.div(index, layout.block), lax.rem(index, layout.block)]
        return pltpu.make_async_copy(held, target, out_sems.at[lax.rem(index, BUFFERS)])

    def is_early(index):
        return (places[index] >= 0) & (places[index] < layout.early)

    def load(index):
        @pl.when(is_early(index))
        def _():
            inward(index).start()

    def store(index):
        @pl.when(is_early(index))
        def _():
            inward(index).wait()
            outward(index, buffers.at[lax.rem(index, BUFFERS)]).start()

        @pl.when(places[index] < 0)
        def _():
            outward(index, blank).start()

    def drain(index):
        @pl.when(places[index] < layout.early)
        def _():
            outward(index, blank).wait()

    ring(layout.peers * layout.block, load, store, drain)


def place_late_kernel(layout, table, perm, me, arrived, held, out, numbers, buffers, in_sems, out_sems):
    page_len = buffers.shape[1]

    def clear(index, carry):
        numbers[index] = -1
        return carry

    lax.fori_loop(0, layout.peers * layout.late, clear, 0)

    def block(source, carry):
        def use(number, code, place):
            @pl.when(place >= layout.early)
            def _():
                numbers[source * layout.late + place - layout.early] = number

        layout.visit(table, perm, source, me[0], page_len, use)
        return carry

    lax.fori_loop(0, layout.peers, block, 0)

    def inward(index):
        spot = lax.rem(index, BUFFERS)
        return pltpu.make_async_copy(
            arrived.at[lax.div(index, layout.late), lax.rem(index, layout.late)],
            buffers.at[spot],
            in_sems.at[spot],
        )

    def outward(index):
        spot = lax.rem(index, BUFFERS)
        target = out.at[lax.div(index, layout.late), jnp.maximum(numbers[index], 0)]
        return pltpu.make_async_copy(buffers.at[spot], target, out_sems.at[spot])

    def load(index):
        @pl.when(numbers[index] >= 0)
        def _():
            inward(index).start()

    def store(index):
        @pl.when(numbers[index] >= 0)
        def _():
            inward(index).wait()
            outward(index).start()

    def drain(index):
        @pl.when(numbers[index] >= 0)
        def _():
            outward(index).wait()

    ring(layout.peers * layout.late, load, store, drain)


def place_early_pages(layout, table, perm, me, arrived, zeros):
    page = arrived.shape[2:]
    return pl.pallas_call(
        lambda *refs: place_kernel(layout, *refs),
        out_shape=jax.ShapeDtypeStruct((layout.peers, layout.block) + page, arrived.dtype),
        grid_spec=pltpu.PrefetchScalarGridSpec(
            num_scalar_prefetch=3,
            grid=(1,),
            in_specs=[pl.BlockSpec(memory_space=pl.ANY)] * 2,
            out_specs=pl.BlockSpec(memory_space=pl.ANY),
            scratch_shapes=scratch(layout, arrived)
            + [pltpu.VMEM(page, arrived.dtype), pltpu.SemaphoreType.DMA],
        ),
        name="place_early",
    )(table, perm, me, arrived, zeros)


def place_late_pages(layout, table, perm, me, arrived, held):
    return pl.pallas_call(
        lambda *refs: place_late_kernel(layout, *refs),
        out_shape=jax.ShapeDtypeStruct(held.shape, held.dtype),
        grid_spec=pltpu.PrefetchScalarGridSpec(
            num_scalar_prefetch=3,
            grid=(1,),
            in_specs=[pl.BlockSpec(memory_space=pl.ANY)] * 2,
            out_specs=pl.BlockSpec(memory_space=pl.ANY),
            scratch_shapes=scratch(layout, arrived),
        ),
        input_output_aliases={4: 0},
        name="place_late",
    )(table, perm, me, arrived, held)


def attend_kernel(lengths, tables, q_ref, nk_ref, nv_ref, *rest):
    k_refs, v_refs = rest[:BLOCK_PAGES], rest[BLOCK_PAGES : 2 * BLOCK_PAGES]
    out_ref, q_rows, top, total, acc = rest[2 * BLOCK_PAGES :]
    kv_heads, rows, head = q_rows.shape
    tokens = q_ref.shape[0]
    groups = rows // tokens
    slot, step = pl.program_id(0), pl.program_id(1)
    page_len = k_refs[0].shape[1]
    block_keys = BLOCK_PAGES * page_len
    length = lengths[slot]
    inv_scale = 1.0 / math.sqrt(head)

    def score(kv, keys):
        return (
            lax.dot_general(
                q_rows[kv], keys, (((1,), (1,)), ((), ())), preferred_element_type=jnp.float32
            )
            * inv_scale
        )

    @pl.when(step == 0)
    def _():
        for kv in range(kv_heads):
            columns = slice(kv * head, (kv + 1) * head)
            for group in range(groups):
                lane = (kv * groups + group) * head
                q_rows[kv, group * tokens : (group + 1) * tokens, :] = q_ref[:, lane : lane + head]
            scores = score(kv, nk_ref[:, columns])
            query_id = lax.broadcasted_iota(jnp.int32, scores.shape, 0) % tokens
            key_id = lax.broadcasted_iota(jnp.int32, scores.shape, 1)
            scores = jnp.where(key_id <= query_id, scores, -1e30)
            highest = jnp.max(scores, axis=-1, keepdims=True)
            weights = jnp.exp(scores - highest)
            top[kv] = jnp.broadcast_to(highest, (rows, head))
            total[kv] = jnp.broadcast_to(jnp.sum(weights, axis=-1, keepdims=True), (rows, head))
            acc[kv] = jnp.dot(
                weights.astype(jnp.bfloat16), nv_ref[:, columns], preferred_element_type=jnp.float32
            )

    @pl.when(step * block_keys < length)
    def _():
        for kv in range(kv_heads):
            columns = slice(kv * head, (kv + 1) * head)
            keys = jnp.concatenate([ref[0, :, columns] for ref in k_refs], axis=0)
            values = jnp.concatenate([ref[0, :, columns] for ref in v_refs], axis=0)
            scores = score(kv, keys)
            key_id = lax.broadcasted_iota(jnp.int32, scores.shape, 1)
            scores = jnp.where(key_id < length - step * block_keys, scores, -1e30)
            before = top[kv]
            highest = jnp.maximum(before, jnp.max(scores, axis=-1, keepdims=True))
            factor = jnp.exp(before - highest)
            weights = jnp.exp(scores - highest[:, :1])
            top[kv] = highest
            total[kv] = total[kv] * factor + jnp.sum(weights, axis=-1, keepdims=True)
            acc[kv] = acc[kv] * factor + jnp.dot(
                weights.astype(jnp.bfloat16), values, preferred_element_type=jnp.float32
            )

    @pl.when(step == pl.num_programs(1) - 1)
    def _():
        for kv in range(kv_heads):
            context = (acc[kv] / total[kv]).astype(jnp.bfloat16)
            for group in range(groups):
                lane = (kv * groups + group) * head
                out_ref[:, lane : lane + head] = context[group * tokens : (group + 1) * tokens]


def attend(lengths, tables, queries, new_keys, new_values, k_pool, v_pool):
    slots, row_pages = tables.shape
    tokens = queries.shape[0] // slots
    page_len, features = k_pool.shape[1:]
    kv_heads = features // HEAD_SIZE
    rows = tokens * (queries.shape[1] // features)
    steps = row_pages // BLOCK_PAGES

    def page_spec(number):
        def pick(slot, step, lengths, tables):
            last = (lengths[slot] + page_len - 1) // page_len - 1
            return (tables[slot * row_pages + jnp.minimum(step * BLOCK_PAGES + number, last)], 0, 0)

        return pl.BlockSpec((1, page_len, features), pick)

    def slot_rows(slot, step, lengths, tables):
        return (slot, 0)

    pages = [page_spec(number) for number in range(BLOCK_PAGES)]
    state = pltpu.VMEM((kv_heads, rows, HEAD_SIZE), jnp.float32)
    return pl.pallas_call(
        attend_kernel,
        out_shape=jax.ShapeDtypeStruct(queries.shape, jnp.bfloat16),
        grid_spec=pltpu.PrefetchScalarGridSpec(
            num_scalar_prefetch=2,
            grid=(slots, steps),
            in_specs=[
                pl.BlockSpec((tokens, queries.shape[1]), slot_rows),
                pl.BlockSpec((tokens, features), slot_rows),
                pl.BlockSpec((tokens, features), slot_rows),
            ]
            + pages
            + pages,
            out_specs=pl.BlockSpec((tokens, queries.shape[1]), slot_rows),
            scratch_shapes=[
                pltpu.VMEM((kv_heads, rows, HEAD_SIZE), jnp.bfloat16),
                state,
                state,
                state,
            ],
        ),
        compiler_params=pltpu.CompilerParams(
            dimension_semantics=("arbitrary", "arbitrary"), vmem_limit_bytes=40 << 20
        ),
        name="attend",
    )(
        lengths,
        tables.reshape(-1),
        queries,
        new_keys,
        new_values,
        *([k_pool] * BLOCK_PAGES),
        *([v_pool] * BLOCK_PAGES),
    )


def shards(hidden, norm_gain, wq, wkv, wo, perm, prior_len, page_table, pool, send_table):
    slots = prior_len.shape[0]
    tokens = hidden.shape[0] // slots
    _, peers, block = send_table.shape
    layout = Layout(slots, page_table.shape[1], peers, block)
    features = pool.shape[-1]
    device = lax.axis_index("req")
    me = device.astype(jnp.int32).reshape(1)
    mine = jnp.concatenate([prior_len, page_table.reshape(-1), send_table.reshape(-1)])
    mine = jnp.pad(mine, (0, layout.width - layout.used)).reshape(-1, 128)
    by_device = exchange(peers, mine)
    table = by_device.reshape(-1)
    by_device = by_device.reshape(peers, layout.width)
    outgoing = pack_pages(layout, table, perm, me, pool)
    arrived = lax.all_to_all(outgoing, "req", split_axis=0, concat_axis=0, tiled=True)

    full_rows = lax.all_gather(hidden, "tp", axis=1, tiled=True)
    late_pool, wkv, outgoing = lax.optimization_barrier((pool, wkv, outgoing))
    requests = lax.dynamic_slice_in_dim(perm, device * slots, slots)
    lengths = by_device[:, :slots].reshape(-1)[requests]
    tables = by_device[:, slots : layout.sends].reshape(-1, layout.row_pages)[requests]

    normalized_input = normalize(full_rows, norm_gain)
    query_proj = jnp.dot(normalized_input, wq, preferred_element_type=jnp.float32)
    pair_proj = jnp.dot(
        normalized_input, wkv.reshape(wkv.shape[0], -1), preferred_element_type=jnp.float32
    )
    positions = (lengths[:, None] + jnp.arange(tokens, dtype=jnp.int32)[None, :]).reshape(-1)
    queries = rotate(query_proj.reshape(query_proj.shape[0], -1, HEAD_SIZE), positions).astype(
        jnp.bfloat16
    )
    pair_heads = pair_proj.reshape(pair_proj.shape[0], 2, -1, HEAD_SIZE)
    new_keys = rotate(pair_heads[:, 0], positions).astype(jnp.bfloat16).reshape(-1, features)
    new_values = pair_heads[:, 1].astype(jnp.bfloat16).reshape(-1, features)
    recent = jnp.stack([new_keys, new_values], axis=1).reshape(slots, tokens, 2, features)
    context = attend(
        lengths,
        tables,
        queries.reshape(queries.shape[0], -1),
        new_keys,
        new_values,
        late_pool[:, :, 0],
        late_pool[:, :, 1],
    )
    partial_value = jnp.dot(context, wo, preferred_element_type=jnp.float32)
    recent, partial_value = lax.optimization_barrier((recent, partial_value))
    attn_out = lax.psum_scatter(
        partial_value.astype(jnp.bfloat16), "tp", scatter_dimension=1, tiled=True
    )
    zeros = jnp.zeros(pool.shape[1:], pool.dtype)
    late_arrived = lax.all_to_all(
        pack_pages(layout, table, perm, me, late_pool, recent, zeros),
        "req",
        split_axis=0,
        concat_axis=0,
        tiled=True,
    )
    early_pages = place_early_pages(layout, table, perm, me, arrived, zeros)
    decode_pages = place_late_pages(layout, table, perm, me, late_arrived, early_pages)
    return (attn_out, decode_pages[None])


def solution(mesh):
    placed = (
        P("req", "tp"),
        P(),
        P(None, "tp"),
        P(None, None, "tp"),
        P("tp", None),
        P(),
        P("req"),
        P("req", None),
        P("req", None, None, "tp"),
        P("req", None, None),
    )
    return jax.shard_map(
        shards,
        mesh=mesh,
        in_specs=placed,
        out_specs=(P("req", "tp"), P("req", None, None, None, None, "tp")),
        check_vma=False,
    )
```

```python
import math

import jax
import jax.numpy as jnp
from jax import lax
from jax.experimental import pallas as pl
from jax.experimental.pallas import tpu as pltpu
from jax.sharding import PartitionSpec as P

HEAD_SIZE = 128
NORM_EPSILON = 1e-05
ROPE_THETA = 100000000.0
BLOCK_PAGES = 4


def normalize(rows, gain):
    wide_rows = rows.astype(jnp.float32)
    mean_square = jnp.mean(wide_rows * wide_rows, axis=-1, keepdims=True)
    return (wide_rows * lax.rsqrt(mean_square + NORM_EPSILON) * gain.astype(jnp.float32)).astype(
        jnp.bfloat16
    )


def rotate(vectors, positions):
    half_size = vectors.shape[-1] // 2
    frequency = jnp.power(
        jnp.float32(ROPE_THETA), -2.0 * jnp.arange(half_size, dtype=jnp.float32) / vectors.shape[-1]
    )
    angles = positions.astype(jnp.float32)[:, None] * frequency[None, :]
    cosine = jnp.cos(angles)[:, None, :]
    sine_part = jnp.sin(angles)[:, None, :]
    first_half = vectors[..., :half_size]
    second_half = vectors[..., half_size:]
    return jnp.concatenate(
        [
            first_half * cosine - second_half * sine_part,
            second_half * cosine + first_half * sine_part,
        ],
        axis=-1,
    )


class Layout:
    def __init__(self, slots, row_pages, peers, block):
        self.slots, self.row_pages, self.peers, self.block = slots, row_pages, peers, block
        self.code_width = row_pages + 1
        self.sends = slots + slots * row_pages
        self.used = self.sends + peers * block
        self.width = -(-self.used // 1024) * 1024
        self.late = 2 * slots
        self.early = block - self.late

    def request(self, perm, device, slot):
        request = perm[device * self.slots + slot]
        return lax.div(request, self.slots) * self.width, lax.rem(request, self.slots)

    def length(self, table, perm, device, slot):
        base, row = self.request(perm, device, slot)
        return table[base + row]

    def physical(self, table, perm, device, slot, page):
        base, row = self.request(perm, device, slot)
        return table[base + self.slots + row * self.row_pages + jnp.minimum(page, self.row_pages - 1)]

    def split(self, code):
        return lax.div(code, self.code_width), lax.rem(code, self.code_width)

    def visit(self, table, perm, source, target, page_len, use):
        whole = [
            lax.div(self.length(table, perm, source, slot), page_len) for slot in range(self.slots)
        ]
        base = source * self.width + self.sends + target * self.block
        plain, tails = jnp.int32(0), jnp.int32(self.block - 1)
        for number in range(self.block):
            code = table[base + number]
            first = whole[0]
            for slot in range(1, self.slots):
                low = slot * self.code_width
                first = jnp.where(code >= low, whole[slot] + low, first)
            valid, tail = code >= 0, code >= first
            place = jnp.where(valid, jnp.where(tail, tails, plain), -1)
            use(number, code, place)
            plain = plain + jnp.where(valid & jnp.logical_not(tail), 1, 0)
            tails = tails - jnp.where(tail, 1, 0)


def exchange_kernel(peers, mine, out, send_sems, recv_sems):
    me = lax.axis_index("req")
    barrier = pltpu.get_barrier_semaphore()
    for hop in range(1, peers):
        pl.semaphore_signal(
            barrier,
            inc=1,
            device_id={"req": lax.rem(me + hop, peers)},
            device_id_type=pl.DeviceIdType.MESH,
        )
    pl.semaphore_wait(barrier, peers - 1)
    copies = []
    for hop in range(1, peers):
        copy = pltpu.make_async_remote_copy(
            src_ref=mine,
            dst_ref=out.at[me],
            send_sem=send_sems.at[hop - 1],
            recv_sem=recv_sems.at[hop - 1],
            device_id={"req": lax.rem(me + hop, peers)},
            device_id_type=pl.DeviceIdType.MESH,
        )
        copy.start()
        copies.append(copy)
    out[me] = mine[...]
    for copy in copies:
        copy.wait()


def exchange(peers, mine):
    return pl.pallas_call(
        lambda *refs: exchange_kernel(peers, *refs),
        out_shape=jax.ShapeDtypeStruct((peers,) + mine.shape, mine.dtype),
        in_specs=[pl.BlockSpec(memory_space=pltpu.VMEM)],
        out_specs=pl.BlockSpec(memory_space=pltpu.VMEM),
        scratch_shapes=[
            pltpu.SemaphoreType.DMA((peers - 1,)),
            pltpu.SemaphoreType.DMA((peers - 1,)),
        ],
        compiler_params=pltpu.CompilerParams(collective_id=0, has_side_effects=True),
        name="exchange",
    )(mine)


BUFFERS = 32
AHEAD = 16


def ring(count, load, store, drain):
    def step(index, carry):
        @pl.when(index < count)
        def _():
            @pl.when(index >= BUFFERS)
            def _():
                drain(index - BUFFERS)

            load(index)

        @pl.when(index >= AHEAD)
        def _():
            store(index - AHEAD)

        return carry

    lax.fori_loop(0, count + AHEAD, step, 0)

    def last(index, carry):
        drain(index)
        return carry

    lax.fori_loop(max(count - BUFFERS, 0), count, last, 0)


def copy_rows(source, source_row, target, target_row, count, sem):
    size = target.shape[0]
    while size:
        offset = lax.div(count, 2 * size) * (2 * size)

        @pl.when(lax.rem(lax.div(count, size), 2) == 1)
        def _(size=size, offset=offset):
            pltpu.make_async_copy(
                source.at[pl.ds(source_row + offset, size)],
                target.at[pl.ds(target_row + offset, size)],
                sem,
            ).start()

        size //= 2


def pack_kernel(layout, late, table, perm, me, pool, *rest):
    if late:
        recent, zeros, out, codes, buffers, in_sems, out_sems = rest
    else:
        out, codes, buffers, in_sems, out_sems = rest
    page_len = buffers.shape[1]
    span = layout.late if late else layout.early
    start = layout.early if late else 0
    count = layout.peers * span

    def clear(index, carry):
        codes[index] = 0
        return carry

    lax.fori_loop(0, count, clear, 0)
    starts = []
    for slot in range(layout.slots):
        base, row = layout.request(perm, me[0], slot)
        starts.append(
            base + layout.slots + row * layout.row_pages - slot * layout.code_width
        )

    def block(target, carry):
        def use(number, code, place):
            inside = (place >= start) & (place < start + span)
            item = code
            if not late:
                origin = starts[0]
                for slot in range(1, layout.slots):
                    origin = jnp.where(code >= slot * layout.code_width, starts[slot], origin)
                item = table[jnp.where(inside, origin + code, 0)]

            @pl.when(inside)
            def _():
                codes[target * span + place - start] = item

        layout.visit(table, perm, me[0], target, page_len, use)
        return carry

    lax.fori_loop(0, layout.peers, block, 0)

    def load(index):
        spot = index & (BUFFERS - 1)
        target, sem = buffers.at[spot], in_sems.at[spot]
        if not late:
            pltpu.make_async_copy(pool.at[codes[index]], target, sem).start()
            return
        slot, page = layout.split(codes[index])
        cached = pool.at[layout.physical(table, perm, me[0], slot, page)]
        length = layout.length(table, perm, me[0], slot)
        full, kept = lax.div(length, page_len), lax.rem(length, page_len)

        @pl.when(page < full)
        def _():
            pltpu.make_async_copy(cached, target, sem).start()

        @pl.when(page == full)
        def _():
            copy_rows(cached, 0, target, 0, kept, sem)
            copy_rows(recent.at[slot], 0, target, kept, page_len - kept, sem)

        @pl.when(page > full)
        def _():
            copy_rows(recent.at[slot], page_len - kept, target, 0, kept, sem)
            copy_rows(zeros, 0, target, kept, page_len - kept, sem)

    def outward(index):
        spot = index & (BUFFERS - 1)
        return pltpu.make_async_copy(buffers.at[spot], out.at[index], out_sems.at[spot])

    def store(index):
        spot = index & (BUFFERS - 1)
        pltpu.make_async_copy(pool.at[0], buffers.at[spot], in_sems.at[spot]).wait()
        outward(index).start()

    ring(count, load, store, lambda index: outward(index).wait())


def scratch(layout, pool):
    return [
        pltpu.SMEM((layout.peers * layout.block,), jnp.int32),
        pltpu.VMEM((BUFFERS,) + pool.shape[-3:], pool.dtype),
        pltpu.SemaphoreType.DMA((BUFFERS,)),
        pltpu.SemaphoreType.DMA((BUFFERS,)),
    ]


def pack_pages(layout, table, perm, me, pool, *fresh):
    late = bool(fresh)
    span = layout.late if late else layout.early
    return pl.pallas_call(
        lambda *refs: pack_kernel(layout, late, *refs),
        out_shape=jax.ShapeDtypeStruct((layout.peers * span,) + pool.shape[1:], pool.dtype),
        grid_spec=pltpu.PrefetchScalarGridSpec(
            num_scalar_prefetch=3,
            grid=(1,),
            in_specs=[pl.BlockSpec(memory_space=pl.ANY)] * (1 + len(fresh)),
            out_specs=pl.BlockSpec(memory_space=pl.ANY),
            scratch_shapes=scratch(layout, pool),
        ),
        name="pack_late" if late else "pack_early",
    )(table, perm, me, pool, *fresh).reshape((layout.peers, span) + pool.shape[1:])


def place_kernel(layout, table, perm, me, arrived, zeros, *rest):
    out, numbers, places, buffers, in_sems, out_sems, blank, blank_sem = rest
    page_len = buffers.shape[1]

    def clear(index, carry):
        numbers[index] = -1
        return carry

    lax.fori_loop(0, layout.peers * layout.late, clear, 0)
    fill = pltpu.make_async_copy(zeros, blank, blank_sem)
    fill.start()

    def block(source, carry):
        def use(number, code, place):
            places[source * layout.block + number] = place

            @pl.when(place >= layout.early)
            def _():
                late_index = source * layout.late + place - layout.early
                numbers[late_index] = source * layout.block + number

        layout.visit(table, perm, source, me[0], page_len, use)
        return carry

    lax.fori_loop(0, layout.peers, block, 0)
    fill.wait()

    def inward(index):
        spot = index & (BUFFERS - 1)
        place = jnp.clip(places[index], 0, layout.early - 1)
        return pltpu.make_async_copy(
            arrived.at[lax.div(index, layout.block), place], buffers.at[spot], in_sems.at[spot]
        )

    def outward(index, held):
        return pltpu.make_async_copy(held, out.at[index], out_sems.at[index & (BUFFERS - 1)])

    def is_early(index):
        return (places[index] >= 0) & (places[index] < layout.early)

    def load(index):
        @pl.when(is_early(index))
        def _():
            inward(index).start()

    def store(index):
        @pl.when(is_early(index))
        def _():
            inward(index).wait()
            outward(index, buffers.at[index & (BUFFERS - 1)]).start()

        @pl.when(places[index] < 0)
        def _():
            outward(index, blank).start()

    def drain(index):
        @pl.when(places[index] < layout.early)
        def _():
            outward(index, blank).wait()

    ring(layout.peers * layout.block, load, store, drain)


def place_late_kernel(count, numbers, arrived, held, out, buffers, in_sems, out_sems):
    def inward(index):
        spot = index & (BUFFERS - 1)
        return pltpu.make_async_copy(arrived.at[index], buffers.at[spot], in_sems.at[spot])

    def outward(index):
        spot = index & (BUFFERS - 1)
        target = out.at[jnp.maximum(numbers[index], 0)]
        return pltpu.make_async_copy(buffers.at[spot], target, out_sems.at[spot])

    def load(index):
        @pl.when(numbers[index] >= 0)
        def _():
            inward(index).start()

    def store(index):
        @pl.when(numbers[index] >= 0)
        def _():
            inward(index).wait()
            outward(index).start()

    def drain(index):
        @pl.when(numbers[index] >= 0)
        def _():
            outward(index).wait()

    ring(count, load, store, drain)


def place_early_pages(layout, table, perm, me, arrived, zeros):
    page = arrived.shape[2:]
    return pl.pallas_call(
        lambda *refs: place_kernel(layout, *refs),
        out_shape=(
            jax.ShapeDtypeStruct((layout.peers * layout.block,) + page, arrived.dtype),
            jax.ShapeDtypeStruct((layout.peers * layout.late,), jnp.int32),
        ),
        grid_spec=pltpu.PrefetchScalarGridSpec(
            num_scalar_prefetch=3,
            grid=(1,),
            in_specs=[pl.BlockSpec(memory_space=pl.ANY)] * 2,
            out_specs=(
                pl.BlockSpec(memory_space=pl.ANY),
                pl.BlockSpec(memory_space=pltpu.SMEM),
            ),
            scratch_shapes=scratch(layout, arrived)
            + [pltpu.VMEM(page, arrived.dtype), pltpu.SemaphoreType.DMA],
        ),
        name="place_early",
    )(table, perm, me, arrived, zeros)


def place_late_pages(numbers, arrived, held):
    arrived = arrived.reshape((-1,) + held.shape[1:])
    return pl.pallas_call(
        lambda *refs: place_late_kernel(arrived.shape[0], *refs),
        out_shape=jax.ShapeDtypeStruct(held.shape, held.dtype),
        grid_spec=pltpu.PrefetchScalarGridSpec(
            num_scalar_prefetch=1,
            grid=(1,),
            in_specs=[pl.BlockSpec(memory_space=pl.ANY)] * 2,
            out_specs=pl.BlockSpec(memory_space=pl.ANY),
            scratch_shapes=[
                pltpu.VMEM((BUFFERS,) + held.shape[1:], held.dtype),
                pltpu.SemaphoreType.DMA((BUFFERS,)),
                pltpu.SemaphoreType.DMA((BUFFERS,)),
            ],
        ),
        input_output_aliases={2: 0},
        name="place_late",
    )(numbers, arrived, held)


def attend_kernel(lengths, tables, q_ref, nk_ref, nv_ref, *rest):
    k_refs, v_refs = rest[:BLOCK_PAGES], rest[BLOCK_PAGES : 2 * BLOCK_PAGES]
    out_ref, q_rows, top, total, acc = rest[2 * BLOCK_PAGES :]
    kv_heads, rows, head = q_rows.shape
    tokens = q_ref.shape[0]
    groups = rows // tokens
    slot, step = pl.program_id(0), pl.program_id(1)
    page_len = k_refs[0].shape[1]
    block_keys = BLOCK_PAGES * page_len
    length = lengths[slot]
    inv_scale = 1.0 / math.sqrt(head)

    def score(kv, keys):
        return (
            lax.dot_general(
                q_rows[kv], keys, (((1,), (1,)), ((), ())), preferred_element_type=jnp.float32
            )
            * inv_scale
        )

    @pl.when(step == 0)
    def _():
        for kv in range(kv_heads):
            columns = slice(kv * head, (kv + 1) * head)
            for group in range(groups):
                lane = (kv * groups + group) * head
                q_rows[kv, group * tokens : (group + 1) * tokens, :] = q_ref[:, lane : lane + head]
            scores = score(kv, nk_ref[:, columns])
            query_id = lax.broadcasted_iota(jnp.int32, scores.shape, 0) % tokens
            key_id = lax.broadcasted_iota(jnp.int32, scores.shape, 1)
            scores = jnp.where(key_id <= query_id, scores, -1e30)
            highest = jnp.max(scores, axis=-1, keepdims=True)
            weights = jnp.exp(scores - highest)
            top[kv] = jnp.broadcast_to(highest, (rows, head))
            total[kv] = jnp.broadcast_to(jnp.sum(weights, axis=-1, keepdims=True), (rows, head))
            acc[kv] = jnp.dot(
                weights.astype(jnp.bfloat16), nv_ref[:, columns], preferred_element_type=jnp.float32
            )

    @pl.when(step * block_keys < length)
    def _():
        for kv in range(kv_heads):
            columns = slice(kv * head, (kv + 1) * head)
            keys = jnp.concatenate([ref[0, :, columns] for ref in k_refs], axis=0)
            values = jnp.concatenate([ref[0, :, columns] for ref in v_refs], axis=0)
            scores = score(kv, keys)
            key_id = lax.broadcasted_iota(jnp.int32, scores.shape, 1)
            scores = jnp.where(key_id < length - step * block_keys, scores, -1e30)
            before = top[kv]
            highest = jnp.maximum(before, jnp.max(scores, axis=-1, keepdims=True))
            factor = jnp.exp(before - highest)
            weights = jnp.exp(scores - highest[:, :1])
            top[kv] = highest
            total[kv] = total[kv] * factor + jnp.sum(weights, axis=-1, keepdims=True)
            acc[kv] = acc[kv] * factor + jnp.dot(
                weights.astype(jnp.bfloat16), values, preferred_element_type=jnp.float32
            )

    @pl.when(step == pl.num_programs(1) - 1)
    def _():
        for kv in range(kv_heads):
            context = (acc[kv] / total[kv]).astype(jnp.bfloat16)
            for group in range(groups):
                lane = (kv * groups + group) * head
                out_ref[:, lane : lane + head] = context[group * tokens : (group + 1) * tokens]


def attend(lengths, tables, queries, new_keys, new_values, k_pool, v_pool):
    slots, row_pages = tables.shape
    tokens = queries.shape[0] // slots
    page_len, features = k_pool.shape[1:]
    kv_heads = features // HEAD_SIZE
    rows = tokens * (queries.shape[1] // features)
    steps = row_pages // BLOCK_PAGES

    def page_spec(number):
        def pick(slot, step, lengths, tables):
            last = (lengths[slot] + page_len - 1) // page_len - 1
            return (tables[slot * row_pages + jnp.minimum(step * BLOCK_PAGES + number, last)], 0, 0)

        return pl.BlockSpec((1, page_len, features), pick)

    def slot_rows(slot, step, lengths, tables):
        return (slot, 0)

    pages = [page_spec(number) for number in range(BLOCK_PAGES)]
    state = pltpu.VMEM((kv_heads, rows, HEAD_SIZE), jnp.float32)
    return pl.pallas_call(
        attend_kernel,
        out_shape=jax.ShapeDtypeStruct(queries.shape, jnp.bfloat16),
        grid_spec=pltpu.PrefetchScalarGridSpec(
            num_scalar_prefetch=2,
            grid=(slots, steps),
            in_specs=[
                pl.BlockSpec((tokens, queries.shape[1]), slot_rows),
                pl.BlockSpec((tokens, features), slot_rows),
                pl.BlockSpec((tokens, features), slot_rows),
            ]
            + pages
            + pages,
            out_specs=pl.BlockSpec((tokens, queries.shape[1]), slot_rows),
            scratch_shapes=[
                pltpu.VMEM((kv_heads, rows, HEAD_SIZE), jnp.bfloat16),
                state,
                state,
                state,
            ],
        ),
        compiler_params=pltpu.CompilerParams(
            dimension_semantics=("arbitrary", "arbitrary"), vmem_limit_bytes=40 << 20
        ),
        name="attend",
    )(
        lengths,
        tables.reshape(-1),
        queries,
        new_keys,
        new_values,
        *([k_pool] * BLOCK_PAGES),
        *([v_pool] * BLOCK_PAGES),
    )


def shards(hidden, norm_gain, wq, wkv, wo, perm, prior_len, page_table, pool, send_table):
    slots = prior_len.shape[0]
    tokens = hidden.shape[0] // slots
    _, peers, block = send_table.shape
    layout = Layout(slots, page_table.shape[1], peers, block)
    features = pool.shape[-1]
    device = lax.axis_index("req")
    me = device.astype(jnp.int32).reshape(1)
    mine = jnp.concatenate([prior_len, page_table.reshape(-1), send_table.reshape(-1)])
    mine = jnp.pad(mine, (0, layout.width - layout.used)).reshape(-1, 128)
    by_device = exchange(peers, mine)
    table = by_device.reshape(-1)
    by_device = by_device.reshape(peers, layout.width)
    outgoing = pack_pages(layout, table, perm, me, pool)
    arrived = lax.all_to_all(outgoing, "req", split_axis=0, concat_axis=0, tiled=True)

    full_rows = lax.all_gather(hidden, "tp", axis=1, tiled=True)
    late_pool, wkv, outgoing = lax.optimization_barrier((pool, wkv, outgoing))
    requests = lax.dynamic_slice_in_dim(perm, device * slots, slots)
    lengths = by_device[:, :slots].reshape(-1)[requests]
    tables = by_device[:, slots : layout.sends].reshape(-1, layout.row_pages)[requests]

    normalized_input = normalize(full_rows, norm_gain)
    query_proj = jnp.dot(normalized_input, wq, preferred_element_type=jnp.float32)
    pair_proj = jnp.dot(
        normalized_input, wkv.reshape(wkv.shape[0], -1), preferred_element_type=jnp.float32
    )
    positions = (lengths[:, None] + jnp.arange(tokens, dtype=jnp.int32)[None, :]).reshape(-1)
    queries = rotate(query_proj.reshape(query_proj.shape[0], -1, HEAD_SIZE), positions).astype(
        jnp.bfloat16
    )
    pair_heads = pair_proj.reshape(pair_proj.shape[0], 2, -1, HEAD_SIZE)
    new_keys = rotate(pair_heads[:, 0], positions).astype(jnp.bfloat16).reshape(-1, features)
    new_values = pair_heads[:, 1].astype(jnp.bfloat16).reshape(-1, features)
    recent = jnp.stack([new_keys, new_values], axis=1).reshape(slots, tokens, 2, features)
    context = attend(
        lengths,
        tables,
        queries.reshape(queries.shape[0], -1),
        new_keys,
        new_values,
        late_pool[:, :, 0],
        late_pool[:, :, 1],
    )
    partial_value = jnp.dot(context, wo, preferred_element_type=jnp.float32)
    recent, partial_value = lax.optimization_barrier((recent, partial_value))
    attn_out = lax.psum_scatter(
        partial_value.astype(jnp.bfloat16), "tp", scatter_dimension=1, tiled=True
    )
    zeros = jnp.zeros(pool.shape[1:], pool.dtype)
    late_arrived = lax.all_to_all(
        pack_pages(layout, table, perm, me, late_pool, recent, zeros),
        "req",
        split_axis=0,
        concat_axis=0,
        tiled=True,
    )
    early_pages, numbers = place_early_pages(layout, table, perm, me, arrived, zeros)
    decode_pages = place_late_pages(numbers, late_arrived, early_pages)
    return (attn_out, decode_pages.reshape((1, peers, block) + pool.shape[1:]))


def solution(mesh):
    placed = (
        P("req", "tp"),
        P(),
        P(None, "tp"),
        P(None, None, "tp"),
        P("tp", None),
        P(),
        P("req"),
        P("req", None),
        P("req", None, None, "tp"),
        P("req", None, None),
    )
    return jax.shard_map(
        shards,
        mesh=mesh,
        in_specs=placed,
        out_specs=(P("req", "tp"), P("req", None, None, None, None, "tp")),
        check_vma=False,
    )
```
